512 devices in a mesh: blk: 128 (over y, z_lo, x, core), head: 4 (over z_hi).
Axes of the slice: x: 4, y: 4, z: 16 (z_hi: 4, z_lo: 4; z = z_hi * 4 + z_lo), core: 2. Of those that a mesh axis runs over, the one named last changes fastest.
Arguments:
- query_states: bfloat16 [128, 2, 64, 2048], P('blk', None, 'head'), may hold values from -24 to 24
- key_states: bfloat16 [128, 2, 64, 512], P('blk', None, None, 'head'), may hold values from -6 to 6
- value_states: bfloat16 [128, 2, 64, 512], P('blk', None, None, 'head'), may hold values from -6 to 6
- doc_lengths: int32 [3], replicated, may hold values from 1 to 12288, 16384 in all
- page_slot: int32 [128, 2, 4], replicated, may hold values from 0 to 2047, as said below
Outputs:
- attended: bfloat16 [128, 2, 64, 2048], P('blk', None, None, 'head')
- kv_cache: bfloat16 [2048, 4, 16, 256], P('blk', 'head')
The draws below stay inside these ranges and needn't reach their ends.
Inputs may be any that keep to these rules, and one draw needn't show every extreme that they name: `page_slot`: all entries differ. The busiest owners hold 16 pages, the least busy 4.
All inputs are finite; a program needn't handle non-finite values.
Results may differ from the reference program's by a relative error of at most 0.007.
Values may be sent and summed in bfloat16 or wider, within the bound.
A program may use at most 64 MiB of HBM per device.

```python
import math
import jax
import jax.numpy as jnp
import numpy as np
from jax import lax

HEADS = 16
KV_HEADS = 4
HEAD_DIM = 128
BLK_TOK = 64
PAGE = 16
DOCS = 3
PAGES_BLK = 4
TOKENS = 16384
LONGEST = 12288
N_BLK = 128


def drawn_parts(key):
    query_key = jax.random.fold_in(key, 11)
    keys_key = jax.random.fold_in(key, 23)
    query_shape = (N_BLK, 2, BLK_TOK, HEADS * HEAD_DIM)
    key_shape = (N_BLK, 2, BLK_TOK, KV_HEADS * HEAD_DIM)
    query_final = jnp.clip(jax.random.normal(query_key, query_shape, jnp.float32), -6.0, 6.0)
    key_final = jnp.clip(jax.random.normal(keys_key, key_shape, jnp.float32), -6.0, 6.0)
    return (query_final, key_final)


def draw_query_states(key, part):
    return drawn_parts(key)[0].astype(jnp.bfloat16)


def draw_key_states(key, part):
    return drawn_parts(key)[1].astype(jnp.bfloat16)


def draw_page_slot(key, part):
    owner_key = jax.random.fold_in(key, 5)
    order_key = jax.random.fold_in(key, 7)
    slot_count = 4 * PAGES_BLK
    all_slots = N_BLK * slot_count
    pattern = jnp.array([4, 4, 2, 2, 1, 1, 1, 1], jnp.int32) * PAGES_BLK
    counts = jax.random.permutation(owner_key, jnp.tile(pattern, N_BLK // 8))
    slot_ids = jnp.arange(all_slots, dtype=jnp.int32)
    unused = (slot_ids % slot_count >= counts[slot_ids // slot_count]).astype(jnp.int32)
    ordering = jnp.argsort(unused * all_slots + slot_ids)
    used_slots = ordering[:N_BLK * 2 * PAGES_BLK].astype(jnp.int32)
    shuffled = jax.random.permutation(order_key, used_slots)
    return shuffled.reshape(N_BLK, 2, PAGES_BLK).astype(jnp.int32)


def shard_levels(rng, dims, cuts, smallest, top_value):
    loudness = 1.0
    for position, shards_of in cuts:
        steps = jax.random.uniform(jax.random.fold_in(jax.random.fold_in(rng, 6), position), (shards_of,), jnp.float32, smallest / len(cuts), top_value / len(cuts))
        loudness = loudness * jnp.repeat(jnp.exp(steps), dims[position] // shards_of).reshape((-1,) + (1,) * (len(dims) - 1 - position))
    return loudness


def length_profile(count, total, bound, slope):
    portions = [(1 << 20) // math.isqrt(standing ** slope) + 1 for standing in range(2, count + 1)]
    spare, given = total - bound - (count - 1), [1] * (count - 1)
    while spare > 0:
        free = [i for i in range(count - 1) if given[i] < bound]
        mass, budget = sum([portions[i] for i in free]), spare
        for i in free:
            addition = min(bound - given[i], max(1, budget * portions[i] // mass), spare)
            given[i] = given[i] + addition
            spare = spare - addition
    return np.array([bound] + given)


def ragged(stream_key, count, total, bound, slope):
    if count == 2:
        one = jax.random.randint(stream_key, (), max(1, total - bound), min(bound, total - 1) + 1)
        return jnp.stack([one, total - one])
    lengths = jnp.asarray(length_profile(count, total, bound, slope), jnp.int32)
    couples = (count - 1) // 2
    giver, receiver = lengths[1:1 + 2 * couples:2], lengths[2:2 + 2 * couples:2]
    slack = jnp.minimum(giver - 1, bound - receiver)
    moved = jax.random.randint(jax.random.fold_in(stream_key, 1), (couples,), 0, 1 << 20) % (slack + 1)
    lengths = lengths.at[1:1 + 2 * couples:2].set(giver - moved).at[2:2 + 2 * couples:2].set(receiver + moved)
    return lengths[jax.random.permutation(jax.random.fold_in(stream_key, 2), count)]


def gaussian(stream_key, shape, scale, reach, shards=(), kind=jnp.bfloat16):
    values = jax.random.normal(stream_key, shape, jnp.float32) * scale
    if len(shards) > 0:
        values = shard_levels(stream_key, shape, shards, -0.22, 0.18) * values
    return jnp.clip(values, min=-reach, max=reach).astype(kind)


def setup_inputs(seed: int = 0) -> dict:
    key_list = jax.random.split(jax.random.key(seed), 6)
    query_states = draw_query_states(jax.random.fold_in(key_list[5], 71), 0)
    key_states = draw_key_states(jax.random.fold_in(key_list[5], 71), 0)
    value_states = gaussian(key_list[2], (N_BLK, 2, BLK_TOK, KV_HEADS * HEAD_DIM), 1.0, 6.0, ((0, 128), (3, 4)))
    doc_lengths = ragged(key_list[3], DOCS, TOKENS, LONGEST, 2).astype(jnp.int32)
    page_slot = draw_page_slot(jax.random.fold_in(key_list[5], 71), 0)
    return {"query_states": query_states, "key_states": key_states, "value_states": value_states, "doc_lengths": doc_lengths, "page_slot": page_slot}


def to_sequence(array):
    first_half = array[:, 0]
    second = array[::-1, 1]
    joined = jnp.concatenate([first_half, second], axis=0)
    return joined.reshape(-1, array.shape[-1])


def from_sequence(matrix, blocks, block_tok):
    shaped = matrix.reshape(2 * blocks, block_tok, matrix.shape[-1])
    return jnp.stack([shaped[:blocks], shaped[blocks:][::-1]], axis=1)


def reference(query_states, key_states, value_states, doc_lengths, page_slot):
    blocks = query_states.shape[0]
    block_tok = query_states.shape[2]
    total_rows = 2 * blocks * block_tok
    group_size = HEADS // KV_HEADS
    seq_q = to_sequence(query_states).reshape(total_rows, KV_HEADS, group_size, HEAD_DIM)
    key_float = to_sequence(key_states).reshape(total_rows, KV_HEADS, HEAD_DIM).astype(jnp.float32)
    value_float = to_sequence(value_states).reshape(total_rows, KV_HEADS, HEAD_DIM).astype(jnp.float32)
    positions = jnp.arange(total_rows, dtype=jnp.int32)
    doc_bounds = jnp.cumsum(doc_lengths)[:-1]
    doc_ids = jnp.sum((positions[:, None] >= doc_bounds[None, :]).astype(jnp.int32), axis=1)
    rows_blk = 8 * block_tok
    block_count = total_rows // rows_blk
    score_scale = HEAD_DIM ** -0.5

    def one_block(block_index):
        first_row = block_index * rows_blk
        q_part = lax.dynamic_slice_in_dim(seq_q, first_row, rows_blk, 0).astype(jnp.float32)
        pos_part = first_row + jnp.arange(rows_blk, dtype=jnp.int32)
        doc_part = lax.dynamic_slice_in_dim(doc_ids, first_row, rows_blk, 0)
        allowed = (positions[None, :] <= pos_part[:, None]) & (doc_ids[None, :] == doc_part[:, None])

        def per_group(group_index):
            query_group = lax.dynamic_index_in_dim(q_part, group_index, 1, keepdims=False)
            key_group = lax.dynamic_index_in_dim(key_float, group_index, 1, keepdims=False)
            value_group = lax.dynamic_index_in_dim(value_float, group_index, 1, keepdims=False)
            scores = jnp.einsum("qhd,kd->qhk", query_group, key_group) * score_scale
            masked = jnp.where(allowed[:, None, :], scores, -1e30)
            running_max = jnp.max(masked, axis=2, keepdims=True)
            weights = jnp.where(allowed[:, None, :], jnp.exp(masked - running_max), 0.0)
            weight_sum = jnp.sum(weights, axis=2)
            rounded = lax.optimization_barrier(weights.astype(jnp.bfloat16)).astype(jnp.float32)
            output = jnp.einsum("qhk,kd->qhd", rounded, value_group) / weight_sum[..., None]
            return output.astype(jnp.bfloat16)

        outputs = lax.map(per_group, jnp.arange(KV_HEADS, dtype=jnp.int32))
        return jnp.moveaxis(outputs, 0, 1).reshape(rows_blk, HEADS * HEAD_DIM)

    pieces_out = lax.map(one_block, jnp.arange(block_count, dtype=jnp.int32))
    attended = from_sequence(pieces_out.reshape(total_rows, HEADS * HEAD_DIM), blocks, block_tok)

    page_count = block_tok // PAGE
    slot_count = 4 * page_count
    key_split = key_states.reshape(blocks, 2, block_tok, KV_HEADS, HEAD_DIM)
    value_split = value_states.reshape(blocks, 2, block_tok, KV_HEADS, HEAD_DIM)
    joined = jnp.concatenate([key_split, value_split], axis=-1)
    page_rows = joined.reshape(blocks, 2, page_count, PAGE, KV_HEADS, 2 * HEAD_DIM)
    page_rows = page_rows.transpose(0, 1, 2, 4, 3, 5).reshape(-1, KV_HEADS, PAGE, 2 * HEAD_DIM)
    kv_cache = jnp.zeros((blocks * slot_count, KV_HEADS, PAGE, 2 * HEAD_DIM), jnp.bfloat16)
    kv_cache = kv_cache.at[page_slot.reshape(-1)].set(page_rows)
    return attended, kv_cache
```

```python
import functools
import jax
import jax.numpy as jnp
from jax import lax
from jax.experimental import pallas as pl
from jax.experimental.pallas import tpu as pltpu
from jax.sharding import PartitionSpec as P

MESH = pl.DeviceIdType.MESH
PAGE = 16
NEG = -1e30
LAG = 4


def order(k):
    return k + k // 2 - 2 * (k // 3)


def kernel(
    q_ref, k_ref, v_ref, doc_ref, slot_ref, out_ref, cache_ref,
    buf, qbuf, qrow, start, qpos, m_s, l_s, acc_s, pages,
    z_recv, a_recv, b_recv, f_recv, d_recv, q_recv, z_send, a_send, b_send, f_send, d_send, q_send,
):
    blk = lax.axis_index("blk")
    head = lax.axis_index("head")
    y, z, x, c = blk // 32, (blk // 8) % 4, (blk // 2) % 4, blk % 2

    def device(yy, zz, xx, cc):
        return (((yy * 4 + zz) * 4 + xx) * 2 + cc, head)

    sibling = device(y, z, x, 1 - c)
    z_peers = [z + 1 - 2 * (z % 2), (z + 2) % 4, 3 - z]

    def remote(src, dst, send, recv, dev):
        return pltpu.make_async_remote_copy(
            src_ref=src, dst_ref=dst, send_sem=send, recv_sem=recv, device_id=dev, device_id_type=MESH
        )

    for half in range(2):
        buf[half, c, y, x, z, 0] = k_ref[0, half].reshape(4, PAGE, 128)
        buf[half, c, y, x, z, 1] = v_ref[0, half].reshape(4, PAGE, 128)

    barrier = pltpu.get_barrier_semaphore()
    peers = [sibling]
    for d in range(1, 4):
        peers.append(device(y, z_peers[d - 1], x, c))
        peers.append(device(y, z, (x + d) % 4, c))
        peers.append(device((y + d) % 4, z, x, c))
        peers.append((blk, (head + d) % 4))
    for dev in peers:
        pl.semaphore_signal(barrier, inc=1, device_id=dev, device_id_type=MESH)
    pl.semaphore_wait(barrier, len(peers))

    for d in range(3):
        unit = buf.at[:, c, y, x, z]
        remote(unit, unit, z_send, z_recv.at[d], device(y, z_peers[d], x, c)).start()

    def send_first(zz):
        for d in (1, 3, 2):
            low = buf.at[0, c, y, x, zz]
            remote(low, low, a_send, a_recv.at[0, d - 1], device(y, z, (x + d) % 4, c)).start()
            high = buf.at[1, c, y, x, zz]
            remote(high, high, a_send, a_recv.at[1, d - 1], device((y + d) % 4, z, x, c)).start()

    send_first(z)

    def query_copy(d):
        to = (head + d) % 4
        return remote(
            q_ref.at[0, :, :, pl.ds(pl.multiple_of(to * 512, 512), 512)],
            qbuf.at[:, pl.ds(pl.multiple_of(head * 16, 16), 16), :],
            q_send, q_recv.at[d - 1], (blk, to),
        )

    for d in range(1, 4):
        query_copy(d).start()
    qbuf[:, pl.ds(pl.multiple_of(head * 16, 16), 16), :] = q_ref[0, :, :, pl.ds(pl.multiple_of(head * 512, 512), 512)]

    bound0 = doc_ref[0]
    bound1 = doc_ref[0] + doc_ref[1]
    for qb in range(2):
        row = lax.broadcasted_iota(jnp.int32, (256, 128), 0) % 64
        pos = row + (blk if qb == 0 else 255 - blk) * 64
        qpos[qb] = pos
        start[qb] = jnp.where(pos >= bound1, bound1, jnp.where(pos >= bound0, bound0, 0))
    m_s[...] = jnp.full_like(m_s, NEG)
    l_s[...] = jnp.zeros_like(l_s)
    acc_s[...] = jnp.zeros_like(acc_s)

    for d in range(3):
        unit = buf.at[:, c, y, x, z_peers[d]]
        remote(unit, unit, z_send, z_recv.at[d], device(y, z_peers[d], x, c)).wait_recv()
        send_first(z_peers[d])

    local = slot_ref[...] - blk * 16
    ident = (
        lax.broadcasted_iota(jnp.int32, local.shape, 0) * 8
        + lax.broadcasted_iota(jnp.int32, local.shape, 1) * 4
        + lax.broadcasted_iota(jnp.int32, local.shape, 2)
        + 1
    )
    for s in range(16):
        pages[s] = jnp.max(jnp.where(local == s, ident, 0))

    def group(g):
        half, p = g % 2, g // 2
        stage = p // 4
        both = (stage + 1) // 2 - 2 * (stage // 3)
        k = (1 - both) * (p % 4) + both * ((p + 12) // 2 - 8)
        b_off = both * (2 * (p % 2) - 1) + 2 * (stage // 3)
        return half, k, order(k), b_off

    def place(half, a_off, b_off):
        yy = (y + 8 + (1 - half) * b_off + half * a_off) % 4
        xx = (x + 8 + half * b_off + (1 - half) * a_off) % 4
        return yy, xx

    def to_sibling(g, half, yy, xx):
        column = buf.at[half, c, yy, xx]
        remote(column, column, d_send, d_recv.at[g], sibling).start()

    scale = 128 ** -0.5 * 1.4426950408889634

    def attend(qb, half, yy, xx):
        keys = buf[half, :, yy, xx, :, 0].reshape(512, 128)
        values = buf[half, :, yy, xx, :, 1].reshape(512, 128)
        scores = lax.dot_general(qrow[qb], keys, (((1,), (1,)), ((), ())), preferred_element_type=jnp.float32)
        lo, hi = start[qb], qpos[qb]
        sign = 1 - 2 * half
        first = half * 255 + sign * (32 * yy + 2 * xx)
        lane = lax.broadcasted_iota(jnp.int32, (1, 128), 1)
        parts = []
        for t in range(4):
            unit = (t // 2) + 8 * (2 * (t % 2) + lane // 64)
            k_pos = (first + sign * unit) * 64 + lane % 64
            part = scores[:, 128 * t : 128 * (t + 1)]
            parts.append(jnp.where((k_pos >= lo) & (k_pos <= hi), part, NEG))
        top = jnp.maximum(jnp.maximum(parts[0], parts[1]), jnp.maximum(parts[2], parts[3]))
        old = m_s[qb]
        new = jnp.maximum(old, jnp.max(top, axis=1, keepdims=True))
        m_s[qb] = new
        factor = jnp.exp2((old - new) * scale)
        weights = [jnp.exp2((part - new) * scale) for part in parts]
        l_s[qb] = l_s[qb] * factor + ((weights[0] + weights[1]) + (weights[2] + weights[3]))
        rounded = jnp.concatenate([w.astype(jnp.bfloat16) for w in weights], axis=1)
        acc_s[qb] = acc_s[qb] * factor + jnp.dot(rounded, values, preferred_element_type=jnp.float32)

    def compute(g):
        half, _, a_off, b_off = group(g)
        yy, xx = place(half, a_off, b_off)
        column = buf.at[half, 1 - c, yy, xx]
        remote(column, column, d_send, d_recv.at[g], sibling).wait_recv()

        @pl.when((half == 0) | (yy >= y))
        def _():
            attend(1, half, yy, xx)

        @pl.when((half == 0) & (yy <= y))
        def _():
            attend(0, half, yy, xx)

    def second_device(half, step):
        yy, xx = place(half, 0, step)
        return device(yy, z, xx, c)

    def first_steps(g, _):
        half, k, a_off, b_off = group(g)
        yy, xx = place(half, a_off, b_off)
        column = buf.at[half, c, yy, xx]

        @pl.when(g >= 2)
        def _():
            remote(column, column, a_send, a_recv.at[half, 3 - a_off], sibling).wait_recv()

        for direction in range(2):
            remote(
                column, column, b_send, b_recv.at[half, k, direction], second_device(half, 1 - 2 * direction)
            ).start()
        to_sibling(g, half, yy, xx)

        @pl.when(g == 1)
        def _():
            for d in range(1, 4):
                query_copy(d).wait_recv()
            for qb in range(2):
                for h in range(4):
                    qrow[qb, 64 * h : 64 * (h + 1)] = qbuf[qb, :, 128 * h : 128 * (h + 1)]

        @pl.when(g >= LAG)
        def _():
            compute(g - LAG)

        return 0

    def second_steps(g, _):
        half, k, a_off, b_off = group(g)
        yy, xx = place(half, a_off, b_off)
        direction = (b_off + 1) // 2
        column = buf.at[half, c, yy, xx]
        remote(column, column, b_send, b_recv.at[half, k, direction], sibling).wait_recv()
        piece = buf.at[half, c, yy, xx, :, direction]
        remote(piece, piece, f_send, f_recv.at[half, k, direction], second_device(half, 1 - 2 * direction)).start()
        to_sibling(g, half, yy, xx)
        compute(g - LAG)
        return 0

    def third_steps(g, _):
        half, k, a_off, b_off = group(g)
        yy, xx = place(half, a_off, b_off)
        for direction in range(2):
            piece = buf.at[half, c, yy, xx, :, direction]
            remote(piece, piece, f_send, f_recv.at[half, k, direction], sibling).wait_recv()
        to_sibling(g, half, yy, xx)
        compute(g - LAG)
        return 0

    def last_steps(g, _):
        compute(g)
        return 0

    lax.fori_loop(0, 8, first_steps, 0)
    lax.fori_loop(8, 24, second_steps, 0)
    lax.fori_loop(24, 32, third_steps, 0)
    lax.fori_loop(32 - LAG, 32, last_steps, 0)

    for qb in range(2):
        for h in range(4):
            rows = slice(64 * h, 64 * (h + 1))
            total = jnp.sum(l_s[qb, rows], axis=1, keepdims=True)
            out_ref[0, qb, :, 128 * h : 128 * (h + 1)] = (acc_s[qb, rows] / total).astype(jnp.bfloat16)

    for s in range(16):
        found = pages[s]
        used = jnp.full((PAGE, 128), found, jnp.int32) > 0
        page = jnp.maximum(found - 1, 0)
        owner, half, n = page // 8, (page // 4) % 2, page % 4
        oy, oz, ox, oc = owner // 32, (owner // 8) % 4, (owner // 2) % 4, owner % 2
        for kv in range(2):
            rows = buf[half, oc, oy, ox, oz, kv, n]
            cache_ref[s, 0, :, 128 * kv : 128 * (kv + 1)] = jnp.where(used, rows, jnp.zeros_like(rows))

    def sent(ref, sem):
        remote(ref, ref, sem, z_recv.at[0], sibling).wait_send()

    sent(buf.at[:, 0, 0, 0, 0:3], z_send)
    sent(buf.at[0, 0, 0:3, 0:2], a_send)
    sent(buf.at[0, 0], b_send)
    sent(buf.at[0, 0, 0:2], f_send)
    sent(buf.at[0], d_send)
    sent(qbuf.at[:, 0:48], q_send)


def per_device(query_states, key_states, value_states, doc_lengths, page_slot):
    vmem = pl.BlockSpec(memory_space=pltpu.VMEM)
    smem = pl.BlockSpec(memory_space=pltpu.SMEM)
    dma = pltpu.SemaphoreType.DMA
    f32 = jnp.float32
    return pl.pallas_call(
        kernel,
        out_shape=(
            jax.ShapeDtypeStruct((1, 2, 64, 512), jnp.bfloat16),
            jax.ShapeDtypeStruct((16, 1, 16, 256), jnp.bfloat16),
        ),
        in_specs=[vmem, vmem, vmem, smem, vmem],
        out_specs=(vmem, vmem),
        scratch_shapes=[
            pltpu.VMEM((2, 2, 4, 4, 4, 2, 4, PAGE, 128), jnp.bfloat16),
            pltpu.VMEM((2, 64, 512), jnp.bfloat16),
            pltpu.VMEM((2, 256, 128), jnp.bfloat16),
            pltpu.VMEM((2, 256, 128), jnp.int32),
            pltpu.VMEM((2, 256, 128), jnp.int32),
            pltpu.VMEM((2, 256, 128), f32),
            pltpu.VMEM((2, 256, 128), f32),
            pltpu.VMEM((2, 256, 128), f32),
            pltpu.SMEM((16,), jnp.int32),
            dma((3,)),
            dma((2, 3)),
            dma((2, 4, 2)),
            dma((2, 4, 2)),
            dma((32,)),
            dma((3,)),
            dma(()), dma(()), dma(()), dma(()), dma(()), dma(()),
        ],
        compiler_params=pltpu.CompilerParams(
            collective_id=0, has_side_effects=True, vmem_limit_bytes=40 * 1024 * 1024
        ),
    )(query_states, key_states, value_states, doc_lengths, page_slot)


def solution(mesh):
    return jax.shard_map(
        per_device,
        mesh=mesh,
        in_specs=(
            P("blk", None, "head", None),
            P("blk", None, None, "head"),
            P("blk", None, None, "head"),
            P(),
            P(),
        ),
        out_specs=(P("blk", None, None, "head"), P("blk", "head", None, None)),
        check_vma=False,
    )
```

```python
import functools
import jax
import jax.numpy as jnp
from jax import lax
from jax.experimental import pallas as pl
from jax.experimental.pallas import tpu as pltpu
from jax.sharding import PartitionSpec as P

MESH = pl.DeviceIdType.MESH
PAGE = 16
NEG = -1e30
LAG = 3
SEND = (3, 2, -1, -1)
NEED = (5, 4, 3, 3)
RATE = 2


def kernel(
    q_ref, k_ref, v_ref, doc_ref, slot_ref, out_ref, cache_ref,
    buf, qbuf, qrow, start, qpos, m_s, l_s, acc_s, pages,
    z_recv, a_recv, b_recv, f_recv, d_recv, q_recv, z_send, a_send, b_send, f_send, d_send, q_send,
    own_sem, go,
):
    blk = lax.axis_index("blk")
    head = lax.axis_index("head")
    y, z, x, c = blk // 32, (blk // 8) % 4, (blk // 2) % 4, blk % 2

    def device(yy, zz, xx, cc):
        return (((yy * 4 + zz) * 4 + xx) * 2 + cc, head)

    sibling = device(y, z, x, 1 - c)
    z_peers = [z + 1 - 2 * (z % 2), (z + 2) % 4, 3 - z]

    def remote(src, dst, send, recv, dev):
        return pltpu.make_async_remote_copy(
            src_ref=src, dst_ref=dst, send_sem=send, recv_sem=recv, device_id=dev, device_id_type=MESH
        )

    def signal(sem, dev):
        pl.semaphore_signal(sem, inc=1, device_id=dev, device_id_type=MESH)

    barrier = pltpu.get_barrier_semaphore()
    for d in range(1, 4):
        signal(barrier, device(y, z_peers[d - 1], x, 0))
        signal(barrier, device(y, z, (x + d) % 4, 0))
        signal(barrier, device((y + d) % 4, z, x, 0))
        signal(barrier, (blk + 1 - c, (head + d) % 4))

    @pl.when(c == 1)
    def _():
        signal(barrier, sibling)

    own = []
    for half in range(2):
        own.append(pltpu.make_async_copy(k_ref.at[half], buf.at[half, c, y, x, z, 0], own_sem.at[2 * half]))
        own.append(pltpu.make_async_copy(v_ref.at[half], buf.at[half, c, y, x, z, 1], own_sem.at[2 * half + 1]))
    own.append(
        pltpu.make_async_copy(
            q_ref.at[0, :, :, pl.ds(pl.multiple_of(head * 512, 512), 512)],
            qbuf.at[:, pl.ds(pl.multiple_of(head * 16, 16), 16), :],
            own_sem.at[4],
        )
    )
    for copy in own:
        copy.start()

    for copy in own:
        copy.wait()

    @pl.when(c == 0)
    def _():
        pl.semaphore_wait(barrier, 19)
        signal(go.at[0], sibling)

    @pl.when(c == 1)
    def _():
        pl.semaphore_wait(go.at[0], 1)

    def query_copy(d):
        to = (head + d) % 4
        return remote(
            q_ref.at[0, :, :, pl.ds(pl.multiple_of(to * 512, 512), 512)],
            qbuf.at[:, pl.ds(pl.multiple_of(head * 16, 16), 16), :],
            q_send, q_recv.at[d - 1], (blk, to),
        )

    def send_queries():
        @pl.when(c == 1)
        def _():
            pl.semaphore_wait(barrier, 6)
            signal(go.at[1], sibling)

        @pl.when(c == 0)
        def _():
            pl.semaphore_wait(go.at[1], 1)

        for d in range(1, 4):
            query_copy(d).start()

    def slice_z(s):
        return (z + 4 + s * (1 - 2 * (z % 2)) * (s % 2) + 2 * (s // 2) * (1 - 2 * (z // 2)) - (s // 3) * 2 * (1 - 2 * (z % 2))) % 4

    def row(half, core, off, zz):
        if half == 0:
            return buf.at[0, core, (y + off) % 4, :, zz]
        return buf.at[1, core, :, (x + off) % 4, zz]

    def part(half, off, zz, kv):
        if half == 0:
            return buf.at[0, c, (y + off) % 4, :, zz, kv]
        return buf.at[1, c, :, (x + off) % 4, zz, kv]

    def second_device(half, step):
        return device((y + step) % 4, z, x, c) if half == 0 else device(y, z, (x + step) % 4, c)

    def to_sibling(half, off, s):
        ref = row(half, c, off, slice_z(s))
        remote(ref, ref, d_send, d_recv.at[s], sibling).start()

    def send_z():
        for d in range(3):
            unit = buf.at[:, c, y, x, z]
            remote(unit, unit, z_send, z_recv.at[d], device(y, z_peers[d], x, c)).start()

    def first_axis(s):
        zz = slice_z(s)
        if not isinstance(s, int):
            unit = buf.at[:, c, y, x, zz]
            remote(unit, unit, z_send, z_recv.at[s - 1], sibling).wait_recv()
        low = buf.at[0, c, y, x, zz]
        high = buf.at[1, c, y, x, zz]
        for d in (1, 3, 2):
            remote(low, low, a_send, a_recv.at[0, s], device(y, z, (x + d) % 4, c)).start()
            remote(high, high, a_send, a_recv.at[1, s], device((y + d) % 4, z, x, c)).start()

    def second_axis(s):
        for half in range(2):
            three = buf.at[0, 0, 0, 0, 0:3]
            remote(three, three, a_send, a_recv.at[half, s], sibling).wait_recv()
            own_row = row(half, c, 0, slice_z(s))
            for direction in range(2):
                remote(
                    own_row, own_row, b_send, b_recv.at[half, s, direction], second_device(half, (1, 3)[direction])
                ).start()
            to_sibling(half, 0, s)

    def forward(s):
        zz = slice_z(s)
        for direction in (1, 0):
            for half in range(2):
                off = (3, 1)[direction]
                got = row(half, c, off, zz)
                remote(got, got, b_send, b_recv.at[half, s, direction], sibling).wait_recv()
                piece = part(half, off, zz, direction)
                remote(piece, piece, f_send, f_recv.at[half, s], second_device(half, (1, 3)[direction])).start()
                to_sibling(half, off, s)

    def far(s):
        for half in range(2):
            got = row(half, c, 2, slice_z(s))
            remote(got, got, f_send, f_recv.at[half, s], sibling).wait_recv()
            to_sibling(half, 2, s)

    send_z()
    first_axis(0)

    @pl.when(head >= 2)
    def _():
        send_queries()


    bound0 = doc_ref[0]
    bound1 = doc_ref[0] + doc_ref[1]
    for qb in range(2):
        token = lax.broadcasted_iota(jnp.int32, (256, 128), 0) % 64
        pos = token + (blk if qb == 0 else 255 - blk) * 64
        qpos[qb] = pos
        start[qb] = jnp.where(pos >= bound1, bound1, jnp.where(pos >= bound0, bound0, 0))
    m_s[...] = jnp.full_like(m_s, NEG)
    l_s[...] = jnp.zeros_like(l_s)
    acc_s[...] = jnp.zeros_like(acc_s)

    local = slot_ref[...] - blk * 16
    ident = (
        lax.broadcasted_iota(jnp.int32, local.shape, 0) * 4
        + lax.broadcasted_iota(jnp.int32, local.shape, 1)
        + lax.broadcasted_iota(jnp.int32, local.shape, 2) * 8
        + 1
    )
    for s in range(16):
        pages[s] = jnp.max(jnp.where(local == s, ident, 0))

    scale = 128 ** -0.5 * 1.4426950408889634

    def attend(s):
        zz = slice_z(s)

        @functools.cache
        def block(i):
            after = lax.div(i + 8 - (y + 1), 8)
            high = lax.div(i + 8 - (y + 5), 8)
            yy = i - after * (y + 1) - high * (4 - y)
            return after, high, yy

        def scores_of(i):
            qb, half, yy = block(i)
            keys = buf[half, :, yy, :, zz, 0].reshape(512, 128)
            return lax.dot_general(qrow[qb], keys, (((1,), (1,)), ((), ())), preferred_element_type=jnp.float32)

        lane = lax.broadcasted_iota(jnp.int32, (1, 128), 1)
        ahead = scores_of(0)
        for i in range(9):
            scores = ahead
            if i < 8:
                ahead = scores_of(i + 1)
            qb, half, yy = block(i)
            sign = 1 - 2 * half
            first = half * 255 + sign * (32 * yy + 8 * zz)
            lo, hi = start[qb], qpos[qb]
            parts = []
            for t in range(4):
                unit = t // 2 + 2 * (2 * (t % 2) + lane // 64)
                k_pos = (first + sign * unit) * 64 + lane % 64
                piece = scores[:, 128 * t : 128 * (t + 1)]
                parts.append(jnp.where((k_pos >= lo) & (k_pos <= hi), piece, NEG))
            top = jnp.maximum(jnp.maximum(parts[0], parts[1]), jnp.maximum(parts[2], parts[3]))
            old = m_s[qb]
            new = jnp.maximum(old, jnp.max(top, axis=1, keepdims=True))
            m_s[qb] = new
            factor = jnp.exp2((old - new) * scale)
            weights = [jnp.exp2((piece - new) * scale) for piece in parts]
            l_s[qb] = l_s[qb] * factor + ((weights[0] + weights[1]) + (weights[2] + weights[3]))
            rounded = jnp.concatenate([w.astype(jnp.bfloat16) for w in weights], axis=1)
            values = buf[half, :, yy, :, zz, 1].reshape(512, 128)
            acc_s[qb] = acc_s[qb] * factor + jnp.dot(rounded, values, preferred_element_type=jnp.float32)

    def compute(s, _):
        whole = buf.at[:, 0, :, :, 0]
        remote(whole, whole, d_send, d_recv.at[s], sibling).wait_recv()
        attend(s)
        return 0

    def by_head(table):
        return table[3] + (table[0] - table[3]) * (1 - (head + 3) // 4) + (table[1] - table[3]) * (head % 3 % 2)

    send_at, need_at = by_head(SEND), by_head(NEED)

    def computed(w):
        return jnp.clip(jnp.minimum(w - LAG, RATE * (w + 1 - need_at)), 0, 4)

    def steps(w, _):
        @pl.when(w < 5)
        def _():
            second_axis(w - 1)

        @pl.when(w < 4)
        def _():
            first_axis(w)

        @pl.when(w == send_at)
        def _():
            send_queries()

        @pl.when((w >= 2) & (w < 6))
        def _():
            forward(w - 2)

        @pl.when((w >= 3) & (w < 7))
        def _():
            far(w - 3)

        @pl.when(w == need_at)
        def _():
            for d in range(1, 4):
                query_copy(d).wait_recv()
            for qb in range(2):
                for h in range(4):
                    qrow[qb, 64 * h : 64 * (h + 1)] = qbuf[qb, :, 128 * h : 128 * (h + 1)]

        lax.fori_loop(computed(w - 1), computed(w), compute, 0)
        return 0

    lax.fori_loop(1, 8, steps, 0)

    for qb in range(2):
        for h in range(4):
            rows = slice(64 * h, 64 * (h + 1))
            total = jnp.sum(l_s[qb, rows], axis=1, keepdims=True)
            out_ref[0, qb, :, 128 * h : 128 * (h + 1)] = (acc_s[qb, rows] / total).astype(jnp.bfloat16)

    for s in range(16):
        found = pages[s]
        used = jnp.full((PAGE, 128), found, jnp.int32) > 0
        page = jnp.maximum(found - 1, 0)
        owner, half, n = page // 8, (page // 4) % 2, page % 4
        oy, oz, ox, oc = owner // 32, (owner // 8) % 4, (owner // 2) % 4, owner % 2
        for kv in range(2):
            rows = buf[half, oc, oy, ox, oz, kv, n]
            cache_ref[s, 0, :, 128 * kv : 128 * (kv + 1)] = jnp.where(used, rows, jnp.zeros_like(rows))

    def sent(ref, sem):
        remote(ref, ref, sem, z_recv.at[0], sibling).wait_send()

    sent(buf.at[:, 0, 0, 0, 0:3], z_send)
    sent(buf.at[0, 0, 0:3, 0:2], a_send)
    sent(buf.at[0, 0], b_send)
    sent(buf.at[0, 0, 0:2], f_send)
    sent(buf.at[0], d_send)
    sent(qbuf.at[:, 0:48], q_send)


def per_device(query_states, key_states, value_states, doc_lengths, page_slot):
    vmem = pl.BlockSpec(memory_space=pltpu.VMEM)
    hbm = pl.BlockSpec(memory_space=pltpu.HBM)
    smem = pl.BlockSpec(memory_space=pltpu.SMEM)
    dma = pltpu.SemaphoreType.DMA
    f32 = jnp.float32
    return pl.pallas_call(
        kernel,
        out_shape=(
            jax.ShapeDtypeStruct((1, 2, 64, 512), jnp.bfloat16),
            jax.ShapeDtypeStruct((16, 1, 16, 256), jnp.bfloat16),
        ),
        in_specs=[hbm, hbm, hbm, smem, vmem],
        out_specs=(vmem, vmem),
        scratch_shapes=[
            pltpu.VMEM((2, 2, 4, 4, 4, 2, 4, PAGE, 128), jnp.bfloat16),
            pltpu.VMEM((2, 64, 512), jnp.bfloat16),
            pltpu.VMEM((2, 256, 128), jnp.bfloat16),
            pltpu.VMEM((2, 256, 128), jnp.int32),
            pltpu.VMEM((2, 256, 128), jnp.int32),
            pltpu.VMEM((2, 256, 128), f32),
            pltpu.VMEM((2, 256, 128), f32),
            pltpu.VMEM((2, 256, 128), f32),
            pltpu.SMEM((16,), jnp.int32),
            dma((3,)),
            dma((2, 4)),
            dma((2, 4, 2)),
            dma((2, 4)),
            dma((4,)),
            dma((3,)),
            dma(()), dma(()), dma(()), dma(()), dma(()), dma(()),
            dma((5,)),
            pltpu.SemaphoreType.REGULAR((2,)),
        ],
        compiler_params=pltpu.CompilerParams(
            collective_id=0, has_side_effects=True, vmem_limit_bytes=62 * 1024 * 1024
        ),
    )(
        query_states,
        key_states.reshape(2, 4, PAGE, 128),
        value_states.reshape(2, 4, PAGE, 128),
        doc_lengths,
        page_slot.transpose(1, 2, 0),
    )


def solution(mesh):
    return jax.shard_map(
        per_device,
        mesh=mesh,
        in_specs=(
            P("blk", None, "head", None),
            P("blk", None, None, "head"),
            P("blk", None, None, "head"),
            P(),
            P(),
        ),
        out_specs=(P("blk", None, None, "head"), P("blk", "head", None, None)),
        check_vma=False,
    )
```

```python
import functools
import jax
import jax.numpy as jnp
from jax import lax
from jax.experimental import pallas as pl
from jax.experimental.pallas import tpu as pltpu
from jax.sharding import PartitionSpec as P

MESH = pl.DeviceIdType.MESH
PAGE = 16
NEG = -1e30
PLAN = (
    (("A", 1), ("B", 0),),
    (("A", 2), ("B", 1), ("F", 0),),
    (("A", 3), ("B", 2), ("F", 1), ("R", 0),),
    (("B", 3), ("F", 2), ("R", 1),),
    (("F", 3), ("R", 2),),
    (("R", 3),),
    (),
)
READY = (2, 3, 4, 6)
SEND = (2, 1, -1, -1)
NEED = (4, 3, 2, 2)
RATE = 2


def kernel(
    q_ref, k_ref, v_ref, doc_ref, slot_ref, out_ref, cache_ref,
    buf, qbuf, qrow, start, qpos, m_s, l_s, acc_s, pages,
    z_recv, a_recv, b_recv, f_recv, d_recv, q_recv, z_send, a_send, b_send, f_send, d_send, q_send,
    own_sem, go,
):
    blk = lax.axis_index("blk")
    head = lax.axis_index("head")
    y, z, x, c = blk // 32, (blk // 8) % 4, (blk // 2) % 4, blk % 2

    def device(yy, zz, xx, cc):
        return (((yy * 4 + zz) * 4 + xx) * 2 + cc, head)

    sibling = device(y, z, x, 1 - c)

    def remote(src, dst, send, recv, dev):
        return pltpu.make_async_remote_copy(
            src_ref=src, dst_ref=dst, send_sem=send, recv_sem=recv, device_id=dev, device_id_type=MESH
        )

    def signal(sem, dev):
        pl.semaphore_signal(sem, inc=1, device_id=dev, device_id_type=MESH)

    barrier = pltpu.get_barrier_semaphore()
    for d in range(1, 4):
        signal(barrier, device(y, z, (x + d) % 4, 0))
        signal(barrier, device((y + d) % 4, z, x, 0))
        signal(barrier, (blk + 1 - c, (head + d) % 4))

    inner = lax.rem(lax.div(z + 1, 2), 2)
    up = 1 - 2 * lax.div(z, 2)
    signal(barrier, device(y, z + up * (1 - 2 * inner), x, 0))

    @pl.when(inner == 1)
    def _():
        signal(barrier, device(y, z + up, x, 0))

    @pl.when(c == 1)
    def _():
        signal(barrier, sibling)

    own = []
    for half in range(2):
        own.append(pltpu.make_async_copy(k_ref.at[half], buf.at[half, c, y, x, z, 0], own_sem.at[2 * half]))
        own.append(pltpu.make_async_copy(v_ref.at[half], buf.at[half, c, y, x, z, 1], own_sem.at[2 * half + 1]))
    own.append(
        pltpu.make_async_copy(
            q_ref.at[0, :, :, pl.ds(pl.multiple_of(head * 512, 512), 512)],
            qbuf.at[:, pl.ds(pl.multiple_of(head * 16, 16), 16), :],
            own_sem.at[4],
        )
    )
    for copy in own:
        copy.start()

    for copy in own:
        copy.wait()

    @pl.when(c == 0)
    def _():
        pl.semaphore_wait(barrier, 15 + 2 * inner)
        signal(go.at[0], sibling)

    @pl.when(c == 1)
    def _():
        pl.semaphore_wait(go.at[0], 1)

    def query_copy(d):
        to = (head + d) % 4
        return remote(
            q_ref.at[0, :, :, pl.ds(pl.multiple_of(to * 512, 512), 512)],
            qbuf.at[:, pl.ds(pl.multiple_of(head * 16, 16), 16), :],
            q_send, q_recv.at[d - 1], (blk, to),
        )

    def send_queries():
        @pl.when(c == 1)
        def _():
            pl.semaphore_wait(barrier, 6)
            signal(go.at[1], sibling)

        @pl.when(c == 0)
        def _():
            pl.semaphore_wait(go.at[1], 1)

        for d in range(1, 4):
            query_copy(d).start()

    def slice_z(s):
        first = 1 - lax.div(s + 3, 4) if not isinstance(s, int) else int(s == 0)
        second = (lax.div(s + 3, 4) - lax.div(s + 2, 4)) if not isinstance(s, int) else int(s == 1)
        step = s + inner * (first - second)
        return (1 - lax.div(z, 2)) * step + lax.div(z, 2) * (3 - step)

    def row(half, core, off, zz):
        if half == 0:
            return buf.at[0, core, (y + off) % 4, :, zz]
        return buf.at[1, core, :, (x + off) % 4, zz]

    def part(half, off, zz, kv):
        if half == 0:
            return buf.at[0, c, (y + off) % 4, :, zz, kv]
        return buf.at[1, c, :, (x + off) % 4, zz, kv]

    def second_device(half, step):
        return device((y + step) % 4, z, x, c) if half == 0 else device(y, z, (x + step) % 4, c)

    def to_sibling(half, off, s):
        ref = row(half, c, off, slice_z(s))
        remote(ref, ref, d_send, d_recv.at[s], sibling).start()

    def z_copy(unit, place, zz):
        return remote(unit, unit, z_send, z_recv.at[place - 1], device(y, zz, x, c))

    def send_z():
        unit = buf.at[:, c, y, x, z]

        @pl.when(inner == 0)
        def _():
            z_copy(unit, 1, z + up).start()

        @pl.when(inner == 1)
        def _():
            z_copy(unit, 1, z - up).start()
            z_copy(unit, 2, z + up).start()

    def first_axis(s):
        zz = slice_z(s)
        if s > 0:
            unit = buf.at[:, c, y, x, zz]
            remote(unit, unit, z_send, z_recv.at[s - 1], sibling).wait_recv()

            @pl.when(inner == (1 if s == 1 else 2))
            def _():
                z_copy(unit, 3, z + up).start()

            @pl.when(inner == (1 if s > 1 else 2))
            def _():
                remote(unit, unit, z_send, z_recv.at[s - 1], device(y, z - up, x, c)).start()

        low = buf.at[0, c, y, x, zz]
        high = buf.at[1, c, y, x, zz]
        for d in (1, 3, 2):
            remote(low, low, a_send, a_recv.at[0, s], device(y, z, (x + d) % 4, c)).start()
            remote(high, high, a_send, a_recv.at[1, s], device((y + d) % 4, z, x, c)).start()

    def second_axis(s):
        for half in range(2):
            three = buf.at[0, 0, 0, 0, 0:3]
            remote(three, three, a_send, a_recv.at[half, s], sibling).wait_recv()
            for first in range(2):
                for direction in range(2):
                    kv = direction if first == 0 else 1 - direction
                    piece = part(half, 0, slice_z(s), kv)
                    remote(
                        piece, piece, b_send, b_recv.at[half, s, direction, kv], second_device(half, (1, 3)[direction])
                    ).start()
            to_sibling(half, 0, s)

    def forward(s):
        zz = slice_z(s)

        def near(half, direction, kv):
            piece = part(half, (3, 1)[direction], zz, kv)
            remote(piece, piece, b_send, b_recv.at[half, s, direction, kv], sibling).wait_recv()
            return piece

        for direction in (1, 0):
            for half in range(2):
                piece = near(half, direction, direction)
                remote(piece, piece, f_send, f_recv.at[half, s], second_device(half, (1, 3)[direction])).start()
        for direction in (1, 0):
            for half in range(2):
                near(half, direction, 1 - direction)
                to_sibling(half, (3, 1)[direction], s)

    def far(s):
        for half in range(2):
            got = row(half, c, 2, slice_z(s))
            remote(got, got, f_send, f_recv.at[half, s], sibling).wait_recv()
            to_sibling(half, 2, s)

    send_z()
    first_axis(0)

    @pl.when(head >= 2)
    def _():
        send_queries()


    bound0 = doc_ref[0]
    bound1 = doc_ref[0] + doc_ref[1]
    for qb in range(2):
        token = lax.broadcasted_iota(jnp.int32, (256, 128), 0) % 64
        pos = token + (blk if qb == 0 else 255 - blk) * 64
        qpos[qb] = pos
        start[qb] = jnp.where(pos >= bound1, bound1, jnp.where(pos >= bound0, bound0, 0))
    m_s[...] = jnp.full_like(m_s, NEG)
    l_s[...] = jnp.zeros_like(l_s)
    acc_s[...] = jnp.zeros_like(acc_s)

    local = slot_ref[...] - blk * 16
    ident = (
        lax.broadcasted_iota(jnp.int32, local.shape, 0) * 4
        + lax.broadcasted_iota(jnp.int32, local.shape, 1)
        + lax.broadcasted_iota(jnp.int32, local.shape, 2) * 8
        + 1
    )
    for s in range(16):
        pages[s] = jnp.max(jnp.where(local == s, ident, 0))

    scale = 128 ** -0.5 * 1.4426950408889634

    def attend(s):
        zz = slice_z(s)

        @functools.cache
        def block(i):
            after = lax.div(i + 8 - (y + 1), 8)
            high = lax.div(i + 8 - (y + 5), 8)
            yy = i - after * (y + 1) - high * (4 - y)
            return after, high, yy

        def scores_of(i):
            qb, half, yy = block(i)
            keys = buf[half, :, yy, :, zz, 0].reshape(512, 128)
            return lax.dot_general(qrow[qb], keys, (((1,), (1,)), ((), ())), preferred_element_type=jnp.float32)

        lane = lax.broadcasted_iota(jnp.int32, (1, 128), 1)
        ahead = scores_of(0)
        for i in range(9):
            scores = ahead
            if i < 8:
                ahead = scores_of(i + 1)
            qb, half, yy = block(i)
            sign = 1 - 2 * half
            first = half * 255 + sign * (32 * yy + 8 * zz)
            lo, hi = start[qb], qpos[qb]
            parts = []
            for t in range(4):
                unit = t // 2 + 2 * (2 * (t % 2) + lane // 64)
                k_pos = (first + sign * unit) * 64 + lane % 64
                piece = scores[:, 128 * t : 128 * (t + 1)]
                parts.append(jnp.where((k_pos >= lo) & (k_pos <= hi), piece, NEG))
            top = jnp.maximum(jnp.maximum(parts[0], parts[1]), jnp.maximum(parts[2], parts[3]))
            old = m_s[qb]
            new = jnp.maximum(old, jnp.max(top, axis=1, keepdims=True))
            m_s[qb] = new
            factor = jnp.exp2((old - new) * scale)
            weights = [jnp.exp2((piece - new) * scale) for piece in parts]
            l_s[qb] = l_s[qb] * factor + ((weights[0] + weights[1]) + (weights[2] + weights[3]))
            rounded = jnp.concatenate([w.astype(jnp.bfloat16) for w in weights], axis=1)
            values = buf[half, :, yy, :, zz, 1].reshape(512, 128)
            acc_s[qb] = acc_s[qb] * factor + jnp.dot(rounded, values, preferred_element_type=jnp.float32)

    def compute(s, _):
        whole = buf.at[:, 0, :, :, 0]
        remote(whole, whole, d_send, d_recv.at[s], sibling).wait_recv()
        attend(s)
        return 0

    def by_head(table):
        return table[3] + (table[0] - table[3]) * (1 - (head + 3) // 4) + (table[1] - table[3]) * (head % 3 % 2)

    send_at, need_at = by_head(SEND), by_head(NEED)

    def computed(w):
        ready = sum(lax.div(w + 16 - at, 16) for at in READY)
        return jnp.clip(jnp.minimum(ready, RATE * (w + 1 - need_at)), 0, 4)

    def steps(w, _):
        for at, list_of in enumerate(PLAN):
            if list_of:

                @pl.when(w == at)
                def _(list_of=list_of):
                    for kind, s in list_of:
                        {"A": first_axis, "B": second_axis, "F": forward, "R": far}[kind](s)

        @pl.when(w == send_at)
        def _():
            send_queries()

        @pl.when(w == need_at)
        def _():
            for d in range(1, 4):
                query_copy(d).wait_recv()
            for qb in range(2):
                for h in range(4):
                    qrow[qb, 64 * h : 64 * (h + 1)] = qbuf[qb, :, 128 * h : 128 * (h + 1)]

        lax.fori_loop(computed(w - 1), computed(w), compute, 0)
        return 0

    lax.fori_loop(0, len(PLAN), steps, 0)

    for qb in range(2):
        for h in range(4):
            rows = slice(64 * h, 64 * (h + 1))
            total = jnp.sum(l_s[qb, rows], axis=1, keepdims=True)
            out_ref[0, qb, :, 128 * h : 128 * (h + 1)] = (acc_s[qb, rows] / total).astype(jnp.bfloat16)

    for s in range(16):
        found = pages[s]
        used = jnp.full((PAGE, 128), found, jnp.int32) > 0
        page = jnp.maximum(found - 1, 0)
        owner, half, n = page // 8, (page // 4) % 2, page % 4
        oy, oz, ox, oc = owner // 32, (owner // 8) % 4, (owner // 2) % 4, owner % 2
        for kv in range(2):
            rows = buf[half, oc, oy, ox, oz, kv, n]
            cache_ref[s, 0, :, 128 * kv : 128 * (kv + 1)] = jnp.where(used, rows, jnp.zeros_like(rows))

    def sent(ref, sem):
        remote(ref, ref, sem, z_recv.at[0], sibling).wait_send()

    sent(buf.at[:, 0, 0, 0, 0:1], z_send)

    @pl.when(inner == 1)
    def _():
        sent(buf.at[:, 0, 0, 0, 0:4], z_send)

    sent(buf.at[0, 0, 0:3, 0:2], a_send)
    sent(buf.at[0, 0], b_send)
    sent(buf.at[0, 0, 0:2], f_send)
    sent(buf.at[0], d_send)
    sent(qbuf.at[:, 0:48], q_send)


def per_device(query_states, key_states, value_states, doc_lengths, page_slot):
    vmem = pl.BlockSpec(memory_space=pltpu.VMEM)
    hbm = pl.BlockSpec(memory_space=pltpu.HBM)
    smem = pl.BlockSpec(memory_space=pltpu.SMEM)
    dma = pltpu.SemaphoreType.DMA
    f32 = jnp.float32
    return pl.pallas_call(
        kernel,
        out_shape=(
            jax.ShapeDtypeStruct((1, 2, 64, 512), jnp.bfloat16),
            jax.ShapeDtypeStruct((16, 1, 16, 256), jnp.bfloat16),
        ),
        in_specs=[hbm, hbm, hbm, smem, vmem],
        out_specs=(vmem, vmem),
        scratch_shapes=[
            pltpu.VMEM((2, 2, 4, 4, 4, 2, 4, PAGE, 128), jnp.bfloat16),
            pltpu.VMEM((2, 64, 512), jnp.bfloat16),
            pltpu.VMEM((2, 256, 128), jnp.bfloat16),
            pltpu.VMEM((2, 256, 128), jnp.int32),
            pltpu.VMEM((2, 256, 128), jnp.int32),
            pltpu.VMEM((2, 256, 128), f32),
            pltpu.VMEM((2, 256, 128), f32),
            pltpu.VMEM((2, 256, 128), f32),
            pltpu.SMEM((16,), jnp.int32),
            dma((3,)),
            dma((2, 4)),
            dma((2, 4, 2, 2)),
            dma((2, 4)),
            dma((4,)),
            dma((3,)),
            dma(()), dma(()), dma(()), dma(()), dma(()), dma(()),
            dma((5,)),
            pltpu.SemaphoreType.REGULAR((2,)),
        ],
        compiler_params=pltpu.CompilerParams(
            collective_id=0, has_side_effects=True, vmem_limit_bytes=62 * 1024 * 1024
        ),
    )(
        query_states,
        key_states.reshape(2, 4, PAGE, 128),
        value_states.reshape(2, 4, PAGE, 128),
        doc_lengths,
        page_slot.transpose(1, 2, 0),
    )


def solution(mesh):
    return jax.shard_map(
        per_device,
        mesh=mesh,
        in_specs=(
            P("blk", None, "head", None),
            P("blk", None, None, "head"),
            P("blk", None, None, "head"),
            P(),
            P(),
        ),
        out_specs=(P("blk", None, None, "head"), P("blk", "head", None, None)),
        check_vma=False,
    )
```

```python
import functools
import jax
import jax.numpy as jnp
from jax import lax
from jax.experimental import pallas as pl
from jax.experimental.pallas import tpu as pltpu
from jax.sharding import PartitionSpec as P

MESH = pl.DeviceIdType.MESH
PAGE = 16
NEG = -1e30
PLAN = (
    (("A", 1), ("B", 0),),
    (("A", 2), ("B", 1), ("F", 0),),
    (("A", 3), ("B", 2), ("F", 1), ("R", 0),),
    (("B", 3), ("F", 2), ("R", 1),),
    (("F", 3), ("R", 2),),
    (("R", 3),),
    (),
)
READY = (3, 4, 5, 6)
SEND = (2, 1, -1, -1)
NEED = (3, 3, 3, 3)
RATE = 2


def kernel(
    q_ref, k_ref, v_ref, doc_ref, slot_ref, out_ref, cache_ref,
    buf, qbuf, qrow, start, qpos, m_s, l_s, acc_s, pages,
    z_recv, a_recv, b_recv, f_recv, d_recv, q_recv, z_send, a_send, b_send, f_send, d_send, q_send,
    own_sem, go,
):
    blk = lax.axis_index("blk")
    head = lax.axis_index("head")
    y, z, x, c = blk // 32, (blk // 8) % 4, (blk // 2) % 4, blk % 2

    def device(yy, zz, xx, cc):
        return (((yy * 4 + zz) * 4 + xx) * 2 + cc, head)

    sibling = device(y, z, x, 1 - c)

    def remote(src, dst, send, recv, dev):
        return pltpu.make_async_remote_copy(
            src_ref=src, dst_ref=dst, send_sem=send, recv_sem=recv, device_id=dev, device_id_type=MESH
        )

    def signal(sem, dev):
        pl.semaphore_signal(sem, inc=1, device_id=dev, device_id_type=MESH)

    barrier = pltpu.get_barrier_semaphore()
    for d in range(1, 4):
        signal(barrier, device(y, z, (x + d) % 4, 0))
        signal(barrier, device((y + d) % 4, z, x, 0))
        signal(barrier, (blk + 1 - c, (head + d) % 4))

    inner = lax.rem(lax.div(z + 1, 2), 2)
    up = 1 - 2 * lax.div(z, 2)
    signal(barrier, device(y, z + up * (1 - 2 * inner), x, 0))

    @pl.when(inner == 1)
    def _():
        signal(barrier, device(y, z + up, x, 0))

    @pl.when(c == 1)
    def _():
        signal(barrier, sibling)

    own = []
    for half in range(2):
        own.append(pltpu.make_async_copy(k_ref.at[half], buf.at[half, c, y, x, z, 0], own_sem.at[2 * half]))
        own.append(pltpu.make_async_copy(v_ref.at[half], buf.at[half, c, y, x, z, 1], own_sem.at[2 * half + 1]))
    own.append(
        pltpu.make_async_copy(
            q_ref.at[0, :, :, pl.ds(pl.multiple_of(head * 512, 512), 512)],
            qbuf.at[:, pl.ds(pl.multiple_of(head * 16, 16), 16), :],
            own_sem.at[4],
        )
    )
    for copy in own:
        copy.start()

    for copy in own:
        copy.wait()

    @pl.when(c == 0)
    def _():
        pl.semaphore_wait(barrier, 15 + 2 * inner)
        signal(go.at[0], sibling)

    @pl.when(c == 1)
    def _():
        pl.semaphore_wait(go.at[0], 1)

    def query_copy(d):
        to = (head + d) % 4
        return remote(
            q_ref.at[0, :, :, pl.ds(pl.multiple_of(to * 512, 512), 512)],
            qbuf.at[:, pl.ds(pl.multiple_of(head * 16, 16), 16), :],
            q_send, q_recv.at[d - 1], (blk, to),
        )

    def send_queries():
        @pl.when(c == 1)
        def _():
            pl.semaphore_wait(barrier, 6)
            signal(go.at[1], sibling)

        @pl.when(c == 0)
        def _():
            pl.semaphore_wait(go.at[1], 1)

        for d in range(1, 4):
            query_copy(d).start()

    def slice_z(s):
        first = 1 - lax.div(s + 3, 4) if not isinstance(s, int) else int(s == 0)
        second = (lax.div(s + 3, 4) - lax.div(s + 2, 4)) if not isinstance(s, int) else int(s == 1)
        step = s + inner * (first - second)
        return (1 - lax.div(z, 2)) * step + lax.div(z, 2) * (3 - step)

    def row(half, core, off, zz):
        if half == 0:
            return buf.at[0, core, (y + off) % 4, :, zz]
        return buf.at[1, core, :, (x + off) % 4, zz]

    def part(half, off, zz, kv):
        if half == 0:
            return buf.at[0, c, (y + off) % 4, :, zz, kv]
        return buf.at[1, c, :, (x + off) % 4, zz, kv]

    def second_device(half, step):
        return device((y + step) % 4, z, x, c) if half == 0 else device(y, z, (x + step) % 4, c)

    def to_sibling(half, off, s):
        ref = row(half, c, off, slice_z(s))
        remote(ref, ref, d_send, d_recv.at[s], sibling).start()

    def z_copy(unit, place, zz):
        return remote(unit, unit, z_send, z_recv.at[place - 1], device(y, zz, x, c))

    def send_z():
        unit = buf.at[:, c, y, x, z]

        @pl.when(inner == 0)
        def _():
            z_copy(unit, 1, z + up).start()

        @pl.when(inner == 1)
        def _():
            z_copy(unit, 1, z - up).start()
            z_copy(unit, 2, z + up).start()

    def first_axis(s):
        zz = slice_z(s)
        if s > 0:
            unit = buf.at[:, c, y, x, zz]
            remote(unit, unit, z_send, z_recv.at[s - 1], sibling).wait_recv()

            @pl.when(inner == (1 if s == 1 else 2))
            def _():
                z_copy(unit, 3, z + up).start()

            @pl.when(inner == (1 if s > 1 else 2))
            def _():
                remote(unit, unit, z_send, z_recv.at[s - 1], device(y, z - up, x, c)).start()

        low = buf.at[0, c, y, x, zz]
        high = buf.at[1, c, y, x, zz]
        for d in (1, 3, 2):
            remote(low, low, a_send, a_recv.at[0, s], device(y, z, (x + d) % 4, c)).start()
            remote(high, high, a_send, a_recv.at[1, s], device((y + d) % 4, z, x, c)).start()

    def second_axis(s):
        for half in range(2):
            three = buf.at[0, 0, 0, 0, 0:3]
            remote(three, three, a_send, a_recv.at[half, s], sibling).wait_recv()
            for first in range(2):
                for direction in range(2):
                    kv = direction if first == 0 else 1 - direction
                    piece = part(half, 0, slice_z(s), kv)
                    remote(
                        piece, piece, b_send, b_recv.at[half, s, direction, kv], second_device(half, (1, 3)[direction])
                    ).start()
            to_sibling(half, 0, s)

    def forward(s):
        zz = slice_z(s)

        def near(half, direction, kv):
            piece = part(half, (3, 1)[direction], zz, kv)
            remote(piece, piece, b_send, b_recv.at[half, s, direction, kv], sibling).wait_recv()
            return piece

        for direction in (1, 0):
            for half in range(2):
                piece = near(half, direction, direction)
                remote(piece, piece, f_send, f_recv.at[half, s], second_device(half, (1, 3)[direction])).start()
        for direction in (1, 0):
            for half in range(2):
                near(half, direction, 1 - direction)
                to_sibling(half, (3, 1)[direction], s)

    def far(s):
        for half in range(2):
            got = row(half, c, 2, slice_z(s))
            remote(got, got, f_send, f_recv.at[half, s], sibling).wait_recv()
            to_sibling(half, 2, s)

    send_z()
    first_axis(0)

    @pl.when(head >= 2)
    def _():
        send_queries()


    bound0 = doc_ref[0]
    bound1 = doc_ref[0] + doc_ref[1]
    for qb in range(2):
        token = lax.broadcasted_iota(jnp.int32, (256, 128), 0) % 64
        pos = token + (blk if qb == 0 else 255 - blk) * 64
        qpos[qb] = pos
        start[qb] = jnp.where(pos >= bound1, bound1, jnp.where(pos >= bound0, bound0, 0))
    m_s[...] = jnp.full_like(m_s, NEG)
    l_s[...] = jnp.zeros_like(l_s)
    acc_s[...] = jnp.zeros_like(acc_s)

    local = slot_ref[...] - blk * 16
    ident = (
        lax.broadcasted_iota(jnp.int32, local.shape, 0) * 4
        + lax.broadcasted_iota(jnp.int32, local.shape, 1)
        + lax.broadcasted_iota(jnp.int32, local.shape, 2) * 8
        + 1
    )
    for s in range(16):
        pages[s] = jnp.max(jnp.where(local == s, ident, 0))

    scale = 128 ** -0.5 * 1.4426950408889634

    def attend(s):
        zz = slice_z(s)

        @functools.cache
        def block(i):
            after = lax.div(i + 8 - (y + 1), 8)
            high = lax.div(i + 8 - (y + 5), 8)
            yy = i - after * (y + 1) - high * (4 - y)
            return after, high, yy

        def scores_of(i):
            qb, half, yy = block(i)
            keys = buf[half, :, yy, :, zz, 0].reshape(512, 128)
            return lax.dot_general(qrow[qb], keys, (((1,), (1,)), ((), ())), preferred_element_type=jnp.float32)

        lane = lax.broadcasted_iota(jnp.int32, (1, 128), 1)
        ahead = scores_of(0)
        for i in range(9):
            scores = ahead
            if i < 8:
                ahead = scores_of(i + 1)
            qb, half, yy = block(i)
            sign = 1 - 2 * half
            first = half * 255 + sign * (32 * yy + 8 * zz)
            lo, hi = start[qb], qpos[qb]
            parts = []
            for t in range(4):
                unit = t // 2 + 2 * (2 * (t % 2) + lane // 64)
                k_pos = (first + sign * unit) * 64 + lane % 64
                piece = scores[:, 128 * t : 128 * (t + 1)]
                parts.append(jnp.where((k_pos >= lo) & (k_pos <= hi), piece, NEG))
            top = jnp.maximum(jnp.maximum(parts[0], parts[1]), jnp.maximum(parts[2], parts[3]))
            old = m_s[qb]
            new = jnp.maximum(old, jnp.max(top, axis=1, keepdims=True))
            m_s[qb] = new
            factor = jnp.exp2((old - new) * scale)
            weights = [jnp.exp2((piece - new) * scale) for piece in parts]
            l_s[qb] = l_s[qb] * factor + ((weights[0] + weights[1]) + (weights[2] + weights[3]))
            rounded = jnp.concatenate([w.astype(jnp.bfloat16) for w in weights], axis=1)
            values = buf[half, :, yy, :, zz, 1].reshape(512, 128)
            acc_s[qb] = acc_s[qb] * factor + jnp.dot(rounded, values, preferred_element_type=jnp.float32)

    def compute(s, _):
        whole = buf.at[:, 0, :, :, 0]
        remote(whole, whole, d_send, d_recv.at[s], sibling).wait_recv()
        attend(s)
        return 0

    def by_head(table):
        return table[3] + (table[0] - table[3]) * (1 - (head + 3) // 4) + (table[1] - table[3]) * (head % 3 % 2)

    send_at, need_at = by_head(SEND), by_head(NEED)

    def computed(w):
        ready = sum(lax.div(w + 16 - at, 16) for at in READY)
        return jnp.clip(jnp.minimum(ready, RATE * (w + 1 - need_at)), 0, 4)

    def steps(w, _):
        for at, list_of in enumerate(PLAN):
            if list_of:

                @pl.when(w == at)
                def _(list_of=list_of):
                    for kind, s in list_of:
                        {"A": first_axis, "B": second_axis, "F": forward, "R": far}[kind](s)

        @pl.when(w == send_at)
        def _():
            send_queries()

        @pl.when(w == need_at)
        def _():
            for d in range(1, 4):
                query_copy(d).wait_recv()
            for qb in range(2):
                for h in range(4):
                    qrow[qb, 64 * h : 64 * (h + 1)] = qbuf[qb, :, 128 * h : 128 * (h + 1)]

        lax.fori_loop(computed(w - 1), computed(w), compute, 0)
        return 0

    lax.fori_loop(0, len(PLAN), steps, 0)

    for qb in range(2):
        for h in range(4):
            rows = slice(64 * h, 64 * (h + 1))
            total = jnp.sum(l_s[qb, rows], axis=1, keepdims=True)
            out_ref[0, qb, :, 128 * h : 128 * (h + 1)] = (acc_s[qb, rows] / total).astype(jnp.bfloat16)

    for s in range(16):
        found = pages[s]
        used = jnp.full((PAGE, 128), found, jnp.int32) > 0
        page = jnp.maximum(found - 1, 0)
        owner, half, n = page // 8, (page // 4) % 2, page % 4
        oy, oz, ox, oc = owner // 32, (owner // 8) % 4, (owner // 2) % 4, owner % 2
        for kv in range(2):
            rows = buf[half, oc, oy, ox, oz, kv, n]
            cache_ref[s, 0, :, 128 * kv : 128 * (kv + 1)] = jnp.where(used, rows, jnp.zeros_like(rows))

    def sent(ref, sem):
        remote(ref, ref, sem, z_recv.at[0], sibling).wait_send()

    sent(buf.at[:, 0, 0, 0, 0:1], z_send)

    @pl.when(inner == 1)
    def _():
        sent(buf.at[:, 0, 0, 0, 0:4], z_send)

    sent(buf.at[0, 0, 0:3, 0:2], a_send)
    sent(buf.at[0, 0], b_send)
    sent(buf.at[0, 0, 0:2], f_send)
    sent(buf.at[0], d_send)
    sent(qbuf.at[:, 0:48], q_send)


def per_device(query_states, key_states, value_states, doc_lengths, page_slot):
    vmem = pl.BlockSpec(memory_space=pltpu.VMEM)
    hbm = pl.BlockSpec(memory_space=pltpu.HBM)
    smem = pl.BlockSpec(memory_space=pltpu.SMEM)
    dma = pltpu.SemaphoreType.DMA
    f32 = jnp.float32
    return pl.pallas_call(
        kernel,
        out_shape=(
            jax.ShapeDtypeStruct((1, 2, 64, 512), jnp.bfloat16),
            jax.ShapeDtypeStruct((16, 1, 16, 256), jnp.bfloat16),
        ),
        in_specs=[hbm, hbm, hbm, smem, vmem],
        out_specs=(vmem, vmem),
        scratch_shapes=[
            pltpu.VMEM((2, 2, 4, 4, 4, 2, 4, PAGE, 128), jnp.bfloat16),
            pltpu.VMEM((2, 64, 512), jnp.bfloat16),
            pltpu.VMEM((2, 256, 128), jnp.bfloat16),
            pltpu.VMEM((2, 256, 128), jnp.int32),
            pltpu.VMEM((2, 256, 128), jnp.int32),
            pltpu.VMEM((2, 256, 128), f32),
            pltpu.VMEM((2, 256, 128), f32),
            pltpu.VMEM((2, 256, 128), f32),
            pltpu.SMEM((16,), jnp.int32),
            dma((3,)),
            dma((2, 4)),
            dma((2, 4, 2, 2)),
            dma((2, 4)),
            dma((4,)),
            dma((3,)),
            dma(()), dma(()), dma(()), dma(()), dma(()), dma(()),
            dma((5,)),
            pltpu.SemaphoreType.REGULAR((2,)),
        ],
        compiler_params=pltpu.CompilerParams(
            collective_id=0, has_side_effects=True, vmem_limit_bytes=62 * 1024 * 1024
        ),
    )(
        query_states,
        key_states.reshape(2, 4, PAGE, 128),
        value_states.reshape(2, 4, PAGE, 128),
        doc_lengths,
        page_slot.transpose(1, 2, 0),
    )


def solution(mesh):
    return jax.shard_map(
        per_device,
        mesh=mesh,
        in_specs=(
            P("blk", None, "head", None),
            P("blk", None, None, "head"),
            P("blk", None, None, "head"),
            P(),
            P(),
        ),
        out_specs=(P("blk", None, None, "head"), P("blk", "head", None, None)),
        check_vma=False,
    )
```
